32 devices in a mesh: row: 4 (over z), col: 8 (over y, x, core).
Axes of the slice: x: 2, y: 2, z: 4, core: 2. Of those that a mesh axis runs over, the one named last changes fastest.
Arguments:
- slab: float32 [4096, 8192], P('row', 'col'), may hold values from -6 to 6
- owner: int32 [2], replicated, may hold values from 0 to 7, as said below
- leaf_reflectors: float32 [2, 4096, 2048], P(None, 'row', 'col'), may hold values from -0.1875 to 0.1875
- leaf_factors: float32 [2, 1024, 2048], P(None, 'row', 'col'), as said below
- tree_reflectors: float32 [2, 2, 1024, 256], P(None, None, 'row'), may hold values from -0.25 to 0.25
- tree_mixers: float32 [2, 2, 1024, 256], P(None, None, 'row'), may hold values from -0.1875 to 0.1875
Outputs:
- updated: float32 [4096, 8192], P('row', 'col')
The draws below stay inside these ranges and needn't reach their ends.
Inputs may be any that keep to these rules, and one draw needn't show every extreme that they name: `owner`: the 2 owners are distinct column blocks, and one of them is the last column block. Every 256 x 256 block of leaf_factors is upper triangular with diagonal entries from 1 to 2.
All inputs are finite; a program needn't handle non-finite values.
Results may differ from the reference program's by a relative error of at most 0.00015.
Values sent between devices are 32-bit elements; how exact they have to be, the bound alone decides.
No kernel may reach another device: no remote copies, remote signals or barrier semaphores. Data moves between devices by JAX's collectives and lax.ppermute only.
A program may use at most 64 MiB of HBM per device.

```python
import jax
import jax.numpy as jnp
import numpy as np
from jax import lax

B = 256
PANELS = 2
ROWS_DEV = 1024
ROWS = 4096
NT = 8192
FACT_ROWS = 1024
CAND_COLS = 2048
LEVELS = 2
N_ROW = 4
N_COL = 8


def draw_owner(key, part):
    order = jax.random.permutation(jax.random.fold_in(key, 7), jnp.arange(N_COL - 1, dtype=jnp.int32))
    chosen = jnp.concatenate([order[:PANELS - 1], jnp.full((1,), N_COL - 1, jnp.int32)])
    offset = jax.random.randint(jax.random.fold_in(key, 11), (), 0, PANELS, dtype=jnp.int32)
    return jnp.roll(chosen, offset).astype(jnp.int32)


def draw_leaf_factors(key, part):
    shape = (PANELS, FACT_ROWS, CAND_COLS)
    first_key, second_key = jax.random.split(key)
    row_pos = lax.broadcasted_iota(jnp.int32, shape, 1) % B
    col_pos = lax.broadcasted_iota(jnp.int32, shape, 2) % B
    upper = jax.random.normal(first_key, shape, jnp.float32) * float(B) ** (-0.5)
    diagonal = jax.random.uniform(second_key, shape, jnp.float32, 1.0, 2.0)
    zeros = jnp.zeros(shape, jnp.float32)
    return jnp.where(col_pos > row_pos, upper, jnp.where(col_pos == row_pos, diagonal, zeros))


def block_scale(stream_key, shape, cuts, low, largest):
    def one(position, shards_of):
        steps = jax.random.uniform(jax.random.fold_in(jax.random.fold_in(stream_key, 6), position), (shards_of,), jnp.float32, low / len(cuts), largest / len(cuts))
        return jnp.repeat(jnp.exp(steps), shape[position] // shards_of).reshape((-1,) + (1,) * (len(shape) - position - 1))

    level = one(*cuts[0])
    for cut in cuts[1:]:
        level = level * one(*cut)
    return level


def scatter_about(key, extent, spread, limit, pieces=(), kind=jnp.bfloat16):
    factor_of = block_scale(key, extent, pieces, -0.22, 0.18) if pieces else 1.0
    array = jax.random.normal(key, extent, jnp.float32) * spread * factor_of
    return jnp.minimum(jnp.maximum(array, -limit), limit).astype(kind)


def setup_inputs(seed: int = 0) -> dict:
    seeds = jax.random.split(jax.random.key(seed), 7)
    return {
        "slab": scatter_about(seeds[0], (ROWS, NT), 1.0, 6.0, ((0, 4), (1, 8)), jnp.float32),
        "owner": draw_owner(jax.random.fold_in(seeds[6], 71), 0),
        "leaf_reflectors": scatter_about(seeds[2], (PANELS, ROWS, CAND_COLS), ROWS_DEV ** -0.5, 0.1875, ((1, 4), (2, 8)), jnp.float32),
        "leaf_factors": draw_leaf_factors(jax.random.fold_in(seeds[6], 71), 0),
        "tree_reflectors": scatter_about(seeds[4], (PANELS, LEVELS, FACT_ROWS, B), (2 * B) ** -0.5, 0.25, ((2, 4),), jnp.float32),
        "tree_mixers": scatter_about(seeds[5], (PANELS, LEVELS, FACT_ROWS, B), (4 * B) ** -0.5, 0.1875, ((2, 4),), jnp.float32),
    }


HIGH = lax.Precision.HIGHEST


def reference(slab, owner, leaf_reflectors, leaf_factors, tree_reflectors, tree_mixers):
    matrix = slab.reshape(N_ROW, ROWS_DEV, NT)
    local_row = jnp.arange(ROWS_DEV)
    for panel_no in range(PANELS):
        col_start = (owner[panel_no] * B).astype(jnp.int32)
        reflect_rows = lax.dynamic_slice_in_dim(leaf_reflectors[panel_no], col_start, B, 1).reshape(N_ROW, ROWS_DEV, B)
        factor_rows = lax.dynamic_slice_in_dim(leaf_factors[panel_no], col_start, B, 1).reshape(N_ROW, B, B)
        reflect_rows = jnp.where((local_row >= panel_no * B)[None, :, None], reflect_rows, jnp.zeros_like(reflect_rows))
        projected = jnp.einsum("rkb,rkn->rbn", reflect_rows, matrix, precision=HIGH)
        scaled = jnp.einsum("rcb,rcn->rbn", factor_rows, projected, precision=HIGH)
        matrix = matrix - jnp.einsum("rkb,rbn->rkn", reflect_rows, scaled, precision=HIGH)
        top_rows = matrix[:, panel_no * B:(panel_no + 1) * B, :]
        for level_no in range(LEVELS):
            partner = np.arange(N_ROW) ^ (1 << level_no)
            halves = tree_reflectors[panel_no, level_no].reshape(N_ROW, B, B)
            mixers = tree_mixers[panel_no, level_no].reshape(N_ROW, B, B)
            partial_sum = jnp.einsum("rcb,rcn->rbn", halves, top_rows, precision=HIGH)
            combined = partial_sum + partial_sum[partner]
            top_rows = top_rows - jnp.einsum("rbc,rcn->rbn", mixers, combined, precision=HIGH)
        matrix = jnp.concatenate([matrix[:, :panel_no * B], top_rows, matrix[:, (panel_no + 1) * B:]], axis=1)
    return matrix.reshape(N_ROW * ROWS_DEV, NT)
```

```python
import jax
import jax.numpy as jnp
from jax import lax
from jax.sharding import PartitionSpec as P

PRECISION = lax.Precision.HIGH
LEADING = (((0,), (0,)), ((), ()))
CHUNKS = 4


def dot(a, b):
    return jnp.dot(a, b, precision=PRECISION, preferred_element_type=jnp.float32)


def dot_t(a, b):
    return lax.dot_general(a, b, LEADING, precision=PRECISION, preferred_element_type=jnp.float32)


def from_partner(shard, apart):
    return lax.ppermute(shard, "row", [(i, i ^ 1 << apart) for i in range(lax.axis_size("row"))])


def swap_cores(shard):
    return lax.ppermute(shard, "col", [(i, i ^ 1) for i in range(lax.axis_size("col"))])


def broadcast_halves(half_0, half_1, owner):
    size = lax.axis_size("col")
    me = lax.axis_index("col")
    first = me % 2 == 0
    arrived = swap_cores(jnp.where(first, half_1, half_0))
    current = jnp.where(me % 2 == owner % 2, jnp.where(first, half_0, half_1), arrived)
    bits = [1 << k for k in range(1, size.bit_length() - 1)]
    turned = bits[len(bits) // 2 :] + bits[: len(bits) // 2]
    for even_bit, odd_bit in zip(bits, turned):
        pairs = [(i, i ^ (odd_bit if i % 2 else even_bit)) for i in range(size)]
        arrived = lax.ppermute(current, "col", pairs)
        bit = jnp.where(first, even_bit, odd_bit)
        current = jnp.where((me ^ owner) & bit == 0, current, arrived)
    other = swap_cores(current)
    return jnp.where(first, current, other), jnp.where(first, other, current)


def broadcast_panel(reflectors, factors, owner, first_row):
    rows = reflectors.shape[0] - first_row
    width = factors.shape[0]
    middle = first_row + rows // 2
    half_0 = jnp.concatenate([reflectors[first_row:middle], factors[: width // 2]], axis=0)
    half_1 = jnp.concatenate([reflectors[middle:], factors[width // 2 :]], axis=0)
    half_0, half_1 = broadcast_halves(half_0, half_1, owner)
    block = jnp.concatenate([half_0[: rows // 2], half_1[: rows // 2]], axis=0)
    factor = jnp.concatenate([half_0[rows // 2 :], half_1[rows // 2 :]], axis=0)
    return block, factor


def shards(slab, owner, leaf_reflectors, leaf_factors, tree_reflectors, tree_mixers):
    rows_dev, columns = slab.shape
    width = leaf_factors.shape[1]
    panels = owner.shape[0]
    levels = lax.axis_size("row").bit_length() - 1
    step = columns // CHUNKS
    lower = slab
    finished = []
    for panel_no in range(panels):
        reflect_rows, factor = broadcast_panel(
            leaf_reflectors[panel_no], leaf_factors[panel_no], owner[panel_no], panel_no * width
        )
        scaled = dot_t(factor, dot_t(reflect_rows, lower))
        top = lower[:width] - dot(reflect_rows[:width], scaled)
        lower = lower[width:] - dot(reflect_rows[width:], scaled)
        pieces = []
        for chunk in range(CHUNKS):
            piece = top[:, chunk * step : (chunk + 1) * step]
            for level_no in range(levels):
                partial_sum = dot_t(tree_reflectors[panel_no, level_no], piece)
                both = partial_sum + from_partner(partial_sum, level_no)
                piece = piece - dot(tree_mixers[panel_no, level_no], both)
            pieces.append(piece)
        finished.append(jnp.concatenate(pieces, axis=1))
    return jnp.concatenate(finished + [lower], axis=0)


def solution(mesh):
    return jax.shard_map(
        shards,
        mesh=mesh,
        in_specs=(
            P("row", "col"),
            P(),
            P(None, "row", "col"),
            P(None, "row", "col"),
            P(None, None, "row", None),
            P(None, None, "row", None),
        ),
        out_specs=P("row", "col"),
        check_vma=False,
    )
```

```python
import jax
import jax.numpy as jnp
from jax import lax
from jax.sharding import PartitionSpec as P

PRECISION = lax.Precision.HIGH
LEADING = (((0,), (0,)), ((), ()))
CUTS = ((1, 1), (1, 1))


def dot(a, b):
    return jnp.dot(a, b, precision=PRECISION, preferred_element_type=jnp.float32)


def dot_t(a, b):
    return lax.dot_general(a, b, LEADING, precision=PRECISION, preferred_element_type=jnp.float32)


def from_partner(shard, apart):
    return lax.ppermute(shard, "row", [(i, i ^ 1 << apart) for i in range(lax.axis_size("row"))])


def swap_cores(shard):
    return lax.ppermute(shard, "col", [(i, i ^ 1) for i in range(lax.axis_size("col"))])


def broadcast_halves(half_0, half_1, owner, held):
    size = lax.axis_size("col")
    me = lax.axis_index("col")
    first = me % 2 == 0
    arrived = swap_cores(jnp.where(first, half_1, half_0))
    if held is not None:
        first_value = held[0, 0]
        owner = owner + (first_value != first_value).astype(owner.dtype)
    marks = [arrived]
    current = jnp.where(me % 2 == owner % 2, jnp.where(first, half_0, half_1), arrived)
    bits = [1 << k for k in range(1, size.bit_length() - 1)]
    turned = bits[len(bits) // 2 :] + bits[: len(bits) // 2]
    for even_bit, odd_bit in zip(bits, turned):
        pairs = [(i, i ^ (odd_bit if i % 2 else even_bit)) for i in range(size)]
        arrived = lax.ppermute(current, "col", pairs)
        bit = jnp.where(first, even_bit, odd_bit)
        current = jnp.where((me ^ owner) & bit == 0, current, arrived)
        marks.append(arrived)
    other = swap_cores(current)
    marks.append(other)
    return jnp.where(first, current, other), jnp.where(first, other, current), marks


def broadcast_panel(reflectors, factors, owner, first_row, held):
    rows = reflectors.shape[0] - first_row
    width = factors.shape[0]
    middle = first_row + rows // 2
    half_0 = jnp.concatenate([reflectors[first_row:middle], factors[: width // 2]], axis=0)
    half_1 = jnp.concatenate([reflectors[middle:], factors[width // 2 :]], axis=0)
    half_0, half_1, marks = broadcast_halves(half_0, half_1, owner, held)
    block = jnp.concatenate([half_0[: rows // 2], half_1[: rows // 2]], axis=0)
    factor = jnp.concatenate([half_0[rows // 2 :], half_1[rows // 2 :]], axis=0)
    return block, factor, marks


def shards(slab, owner, leaf_reflectors, leaf_factors, tree_reflectors, tree_mixers):
    rows_dev, columns = slab.shape
    width = leaf_factors.shape[1]
    panels = owner.shape[0]
    levels = lax.axis_size("row").bit_length() - 1
    held = None
    lower = slab
    finished = []
    for panel_no in range(panels):
        reflect_rows, factor, marks = broadcast_panel(
            leaf_reflectors[panel_no], leaf_factors[panel_no], owner[panel_no], panel_no * width, held
        )
        held = marks[-2]
        scaled = dot_t(factor, dot_t(reflect_rows, lower))
        top = lower[:width] - dot(reflect_rows[:width], scaled)
        lower = lower[width:] - dot(reflect_rows[width:], scaled)
        pieces = []
        parts = CUTS[min(panel_no, len(CUTS) - 1)]
        start = 0
        for part in parts:
            step = columns * part // sum(parts)
            piece = top[:, start : start + step]
            start += step
            for level_no in range(levels):
                partial_sum = dot_t(tree_reflectors[panel_no, level_no], piece)
                both = partial_sum + from_partner(partial_sum, level_no)
                piece = piece - dot(tree_mixers[panel_no, level_no], both)
            pieces.append(piece)
        finished.append(jnp.concatenate(pieces, axis=1))
    return jnp.concatenate(finished + [lower], axis=0)


def solution(mesh):
    return jax.shard_map(
        shards,
        mesh=mesh,
        in_specs=(
            P("row", "col"),
            P(),
            P(None, "row", "col"),
            P(None, "row", "col"),
            P(None, None, "row", None),
            P(None, None, "row", None),
        ),
        out_specs=P("row", "col"),
        check_vma=False,
    )
```

```python
import jax
import jax.numpy as jnp
from jax import lax
from jax.sharding import PartitionSpec as P

PRECISION = lax.Precision.HIGH
LEADING = (((0,), (0,)), ((), ()))
CUTS = ((1, 1), (1, 1))
STREAMS = 1
GATE_0 = "none"
GATE_1 = "arrived"
GATE_2 = "own"
GATE_3 = "own"
FIRST_AFTER = False
ALONE = False
UPDATE = True


def dot(a, b):
    return jnp.dot(a, b, precision=PRECISION, preferred_element_type=jnp.float32)


def dot_t(a, b):
    return lax.dot_general(a, b, LEADING, precision=PRECISION, preferred_element_type=jnp.float32)


def from_partner(shard, apart):
    return lax.ppermute(shard, "row", [(i, i ^ 1 << apart) for i in range(lax.axis_size("row"))])


def swap_cores(shard):
    return lax.ppermute(shard, "col", [(i, i ^ 1) for i in range(lax.axis_size("col"))])


def never(held, columns):
    row = held[:1, :columns]
    return row != row


def after(value, held):
    if held is None:
        return value
    return jnp.where(never(held, value.shape[1]), -value, value)


class Broadcast:
    def __init__(self, reflectors, factors, owner, first_row, streams):
        size = lax.axis_size("col")
        self.me = lax.axis_index("col")
        self.first = self.me % 2 == 0
        self.owner = owner
        self.rows = reflectors.shape[0] - first_row
        self.width = factors.shape[0]
        middle = first_row + self.rows // 2
        block_0 = jnp.concatenate([reflectors[first_row:middle], factors[: self.width // 2]], axis=0)
        block_1 = jnp.concatenate([reflectors[middle:], factors[self.width // 2 :]], axis=0)
        part = block_0.shape[0] // streams
        cut = [slice(s * part, (s + 1) * part) for s in range(streams)]
        self.halves = [(block_0[c], block_1[c]) for c in cut]
        bits = [1 << k for k in range(1, size.bit_length() - 1)]
        turned = bits[len(bits) // 2 :] + bits[: len(bits) // 2]
        self.exchanges = [
            (
                [(i, i ^ (odd if i % 2 else even)) for i in range(size)],
                jnp.where(self.first, even, odd),
            )
            for even, odd in zip(bits, turned)
        ]
        self.bit = 1

    def begin(self, held=None):
        sent = [after(jnp.where(self.first, h1, h0), held) for h0, h1 in self.halves]
        self.arrived = [swap_cores(s) for s in sent]
        self.current = [jnp.where(self.first, h0, h1) for h0, h1 in self.halves]

    def select(self, held):
        keep = (self.me ^ self.owner) & self.bit == 0
        result = []
        for current, arrived in zip(self.current, self.arrived):
            if held is not None:
                keep = jnp.logical_or(keep, never(held, current.shape[1]))
            result.append(jnp.where(keep, current, arrived))
        self.current = result

    def exchange(self, number, held=None):
        self.select(held)
        pairs, self.bit = self.exchanges[number]
        self.arrived = [lax.ppermute(c, "col", pairs) for c in self.current]

    def end(self, held=None):
        self.select(held)
        other = [swap_cores(c) for c in self.current]
        self.arrived = other
        side_0 = jnp.concatenate([jnp.where(self.first, c, o) for c, o in zip(self.current, other)], axis=0)
        side_1 = jnp.concatenate([jnp.where(self.first, o, c) for c, o in zip(self.current, other)], axis=0)
        half = self.rows // 2
        block = jnp.concatenate([side_0[:half], side_1[:half]], axis=0)
        return block, jnp.concatenate([side_0[half:], side_1[half:]], axis=0)


def shards(slab, owner, leaf_reflectors, leaf_factors, tree_reflectors, tree_mixers):
    rows_dev, columns = slab.shape
    width = leaf_factors.shape[1]
    panels = owner.shape[0]
    levels = lax.axis_size("row").bit_length() - 1

    def bounds(panel_no):
        parts = CUTS[min(panel_no, len(CUTS) - 1)]
        edges = [0]
        for part in parts:
            edges.append(edges[-1] + columns * part // sum(parts))
        return list(zip(edges[:-1], edges[1:]))

    casts = [
        Broadcast(
            leaf_reflectors[p], leaf_factors[p], owner[p], p * width, 1 if p else STREAMS
        )
        for p in range(panels)
    ]
    lower = slab
    tops, chunks = [], []
    marks = {"none": None}
    for panel_no, cast in enumerate(casts):
        later = panel_no > 0
        cast.begin(marks[GATE_0] if later else None)
        for number in range(len(cast.exchanges)):
            cast.exchange(number, (marks[GATE_1] if number == 0 else marks[GATE_2]) if later else None)
            if number == len(cast.exchanges) - 1:
                marks["arrived"] = cast.arrived[-1]
            if number == 0:
                marks["arrived_first"] = cast.arrived[-1]
        block, factor = cast.end(marks[GATE_3] if later else None)
        marks["other"] = cast.arrived[-1]
        scaled = dot_t(factor, dot_t(block, lower))
        top = lower[:width] - dot(block[:width], scaled)
        lower = lower[width:] - dot(block[width:], scaled)
        tops.append(top)
        row = []
        for start, stop in bounds(panel_no):
            piece = top[:, start:stop]
            own = dot_t(tree_reflectors[panel_no, 0], piece)
            if ALONE and row:
                own = after(own, row[0][2])
            row.append([piece, own, from_partner(own, 0)])
        chunks.append(row)
        marks["own"] = row[0][1]
        marks["theirs"] = row[0][2]
    for panel_no in range(panels):
        for level_no in range(levels - 1):
            for chunk in chunks[panel_no]:
                piece, own, theirs = chunk
                both = own + theirs
                if FIRST_AFTER and panel_no == 0:
                    both = after(both, chunks[1][0][1])
                piece = piece - dot(tree_mixers[panel_no, level_no], both)
                own = dot_t(tree_reflectors[panel_no, level_no + 1], piece)
                chunk[:] = [piece, own, from_partner(own, level_no + 1)]
    if UPDATE:
        result = jnp.concatenate(tops + [lower], axis=0)
    else:
        rows_out = []
    for panel_no in range(panels):
        pieces = []
        for (start, stop), (piece, own, theirs) in zip(bounds(panel_no), chunks[panel_no]):
            piece = piece - dot(tree_mixers[panel_no, levels - 1], own + theirs)
            if UPDATE:
                result = lax.dynamic_update_slice(result, piece, (panel_no * width, start))
            pieces.append(piece)
        if not UPDATE:
            rows_out.append(jnp.concatenate(pieces, axis=1))
    if not UPDATE:
        result = jnp.concatenate(rows_out + [lower], axis=0)
    return result


def solution(mesh):
    return jax.shard_map(
        shards,
        mesh=mesh,
        in_specs=(
            P("row", "col"),
            P(),
            P(None, "row", "col"),
            P(None, "row", "col"),
            P(None, None, "row", None),
            P(None, None, "row", None),
        ),
        out_specs=P("row", "col"),
        check_vma=False,
    )
```

```python
import jax
import jax.numpy as jnp
from jax import lax
from jax.sharding import PartitionSpec as P

PRECISION = lax.Precision.HIGH
LEADING = (((0,), (0,)), ((), ()))
CUTS = ((1, 1, 1, 1), (1, 1))
STREAMS = 1
DYNAMIC = True
PLAN = (
    ("begin0", ""),
    ("move0.0", ""),
    ("move0.1", ""),
    ("end0", ""),
    ("send0.0", ""),
    ("leaf0", ""),
    ("send0.1", ""),
    ("send0.2", "got0.0"),
    ("send0.3", "got0.0"),
    ("begin1", ""),
    ("move1.0", "own0.0"),
    ("move1.1", ""),
    ("end1", ""),
    ("leaf1", ""),
    ("send1.0", ""),
    ("send1.1", "got1.0"),
    ("tree0.0", ""),
    ("tree0.1", "own0.3"),
    ("tree0.2", ""),
    ("tree0.3", "own1.0"),
    ("tree1.0", ""),
    ("tree1.1", ""),
    ("last0.0", ""),
    ("last0.1", ""),
    ("last0.2", ""),
    ("last0.3", ""),
    ("last1.0", ""),
    ("last1.1", ""),
)


def dot(a, b):
    return jnp.dot(a, b, precision=PRECISION, preferred_element_type=jnp.float32)


def dot_t(a, b):
    return lax.dot_general(a, b, LEADING, precision=PRECISION, preferred_element_type=jnp.float32)


def from_partner(shard, apart):
    return lax.ppermute(shard, "row", [(i, i ^ 1 << apart) for i in range(lax.axis_size("row"))])


def swap_cores(shard):
    return lax.ppermute(shard, "col", [(i, i ^ 1) for i in range(lax.axis_size("col"))])


def never(held, columns):
    row = held[:1, : min(columns, held.shape[1])]
    if columns > row.shape[1]:
        row = jnp.tile(row, (1, columns // row.shape[1]))
    return row != row


def after(value, held):
    if held is None:
        return value
    return jnp.where(never(held, value.shape[1]), -value, value)


class Broadcast:
    def __init__(self, reflectors, factors, owner, first_row, streams):
        size = lax.axis_size("col")
        self.me = lax.axis_index("col")
        self.first = self.me % 2 == 0
        self.owner = owner
        self.rows = reflectors.shape[0] - first_row
        self.width = factors.shape[0]
        middle = first_row + self.rows // 2
        part = (self.rows + self.width) // 2 // streams
        cut = [slice(k * part, (k + 1) * part) for k in range(streams)]
        if DYNAMIC:

            def half(number):
                rows = lax.dynamic_slice_in_dim(
                    reflectors, first_row + number * (self.rows // 2), self.rows // 2, 0
                )
                factor = lax.dynamic_slice_in_dim(factors, number * (self.width // 2), self.width // 2, 0)
                return jnp.concatenate([rows, factor], axis=0)

            mine = half(self.me % 2)
            other = half(1 - self.me % 2)
        else:
            block_0 = jnp.concatenate([reflectors[first_row:middle], factors[: self.width // 2]], axis=0)
            block_1 = jnp.concatenate([reflectors[middle:], factors[self.width // 2 :]], axis=0)
            mine = jnp.where(self.first, block_0, block_1)
            other = jnp.where(self.first, block_1, block_0)
        self.mine, self.sent = [mine[c] for c in cut], [other[c] for c in cut]
        bits = [1 << k for k in range(1, size.bit_length() - 1)]
        turned = bits[len(bits) // 2 :] + bits[: len(bits) // 2]
        self.exchanges = [
            (
                [(i, i ^ (odd if i % 2 else even)) for i in range(size)],
                jnp.where(self.first, even, odd),
            )
            for even, odd in zip(bits, turned)
        ]
        self.bit = 1

    def begin(self, held=None):
        self.arrived = [swap_cores(after(s, held)) for s in self.sent]
        self.current = self.mine

    def select(self, held):
        keep = (self.me ^ self.owner) & self.bit == 0
        result = []
        for current, arrived in zip(self.current, self.arrived):
            if held is not None:
                keep = jnp.logical_or(keep, never(held, current.shape[1]))
            result.append(jnp.where(keep, current, arrived))
        self.current = result

    def exchange(self, number, held=None):
        self.select(held)
        pairs, self.bit = self.exchanges[number]
        self.arrived = [lax.ppermute(c, "col", pairs) for c in self.current]

    def end(self, held=None):
        self.select(held)
        other = [swap_cores(c) for c in self.current]
        self.arrived = other
        side_0 = jnp.concatenate([jnp.where(self.first, c, o) for c, o in zip(self.current, other)], axis=0)
        side_1 = jnp.concatenate([jnp.where(self.first, o, c) for c, o in zip(self.current, other)], axis=0)
        half = self.rows // 2
        block = jnp.concatenate([side_0[:half], side_1[:half]], axis=0)
        return block, jnp.concatenate([side_0[half:], side_1[half:]], axis=0)


def shards(slab, owner, leaf_reflectors, leaf_factors, tree_reflectors, tree_mixers):
    rows_dev, columns = slab.shape
    width = leaf_factors.shape[1]
    panels = owner.shape[0]
    levels = lax.axis_size("row").bit_length() - 1

    def bounds(panel_no):
        parts = CUTS[min(panel_no, len(CUTS) - 1)]
        edges = [0]
        for part in parts:
            edges.append(edges[-1] + columns * part // sum(parts))
        return list(zip(edges[:-1], edges[1:]))

    casts = [
        Broadcast(
            leaf_reflectors[p], leaf_factors[p], owner[p], p * width, 1 if p else STREAMS
        )
        for p in range(panels)
    ]
    blocks = [None] * panels
    tops = [None] * panels
    chunks = [{} for _ in range(panels)]
    edges = [bounds(p) for p in range(panels)]
    marks = {}
    lower = [slab]
    result = None

    def leaf(panel_no):
        block, factor = blocks[panel_no]
        matrix = lower[-1]
        scaled = dot_t(factor, dot_t(block, matrix))
        tops[panel_no] = matrix[:width] - dot(block[:width], scaled)
        lower.append(matrix[width:] - dot(block[width:], scaled))

    def head(panel_no, chunk):
        block, factor = blocks[panel_no]
        start, stop = edges[panel_no][chunk]
        part = lower[-1][:, start:stop]
        scaled = dot_t(factor, dot_t(block, part))
        return part[:width] - dot(block[:width], scaled)

    def send(panel_no, chunk, held):
        start, stop = edges[panel_no][chunk]
        piece = head(panel_no, chunk) if tops[panel_no] is None else tops[panel_no][:, start:stop]
        own = after(dot_t(tree_reflectors[panel_no, 0], piece), held)
        theirs = from_partner(own, 0)
        chunks[panel_no][chunk] = [piece, own, theirs, 0]
        marks[f"own{panel_no}.{chunk}"] = own
        marks[f"got{panel_no}.{chunk}"] = theirs

    def tree(panel_no, chunk, held):
        piece, own, theirs, level_no = chunks[panel_no][chunk]
        piece = piece - dot(tree_mixers[panel_no, level_no], after(own + theirs, held))
        own = dot_t(tree_reflectors[panel_no, level_no + 1], piece)
        theirs = from_partner(own, level_no + 1)
        chunks[panel_no][chunk] = [piece, own, theirs, level_no + 1]
        marks[f"up{panel_no}.{chunk}"] = own
        marks[f"gup{panel_no}.{chunk}"] = theirs

    def last(panel_no, chunk, held):
        nonlocal result
        if result is None:
            result = jnp.concatenate(tops + lower[-1:], axis=0)
        piece, own, theirs, level_no = chunks[panel_no][chunk]
        piece = piece - dot(tree_mixers[panel_no, level_no], after(own + theirs, held))
        marks[f"end{panel_no}.{chunk}"] = piece
        result = lax.dynamic_update_slice(result, piece, (panel_no * width, edges[panel_no][chunk][0]))

    for text, mark in PLAN:
        held = marks[mark] if mark else None
        name, numbers = text.rstrip("0123456789."), text[len(text.rstrip("0123456789.")) :].split(".")
        panel_no = int(numbers[0])
        if panel_no >= panels:
            continue
        if name == "begin":
            casts[panel_no].begin(held)
        elif name == "move":
            if int(numbers[1]) == 0:
                casts[panel_no].exchange(0, held)
                marks[f"arr{panel_no}.0"] = casts[panel_no].arrived[-1]
            else:
                for number in range(1, len(casts[panel_no].exchanges)):
                    casts[panel_no].exchange(number, held)
                marks[f"arr{panel_no}.1"] = casts[panel_no].arrived[-1]
        elif name == "end":
            blocks[panel_no] = casts[panel_no].end(held)
            marks[f"arr{panel_no}.2"] = casts[panel_no].arrived[-1]
        elif name == "leaf":
            leaf(panel_no)
        elif name == "send":
            send(panel_no, int(numbers[1]), held)
        elif name == "tree":
            for _ in range(levels - 1):
                tree(panel_no, int(numbers[1]), held)
        else:
            last(panel_no, int(numbers[1]), held)
    return result


def solution(mesh):
    return jax.shard_map(
        shards,
        mesh=mesh,
        in_specs=(
            P("row", "col"),
            P(),
            P(None, "row", "col"),
            P(None, "row", "col"),
            P(None, None, "row", None),
            P(None, None, "row", None),
        ),
        out_specs=P("row", "col"),
        check_vma=False,
    )
```

```python
import jax
import jax.numpy as jnp
from jax import lax
from jax.sharding import PartitionSpec as P

PRECISION = lax.Precision.HIGH
LEADING = (((0,), (0,)), ((), ()))
CUTS = ((1, 1, 1, 1), (1, 1))
STREAMS = 2
PLAN = (
    ("begin0", ""),
    ("move0.0", ""),
    ("move0.1", ""),
    ("end0", ""),
    ("send0.0", ""),
    ("leaf0", "own0.0"),
    ("send0.1", ""),
    ("send0.2", "got0.0"),
    ("send0.3", "got0.0"),
    ("begin1", ""),
    ("move1.0", "own0.0"),
    ("move1.1", ""),
    ("end1", ""),
    ("leaf1", ""),
    ("send1.0", ""),
    ("send1.1", "got1.0"),
    ("tree0.0", ""),
    ("tree0.1", "own0.3"),
    ("tree0.2", ""),
    ("tree0.3", "own1.0"),
    ("tree1.0", ""),
    ("tree1.1", ""),
    ("last0.0", ""),
    ("last0.1", ""),
    ("last0.2", ""),
    ("last0.3", ""),
    ("last1.0", ""),
    ("last1.1", ""),
)


def dot(a, b):
    return jnp.dot(a, b, precision=PRECISION, preferred_element_type=jnp.float32)


def dot_t(a, b):
    return lax.dot_general(a, b, LEADING, precision=PRECISION, preferred_element_type=jnp.float32)


def from_partner(shard, apart):
    return lax.ppermute(shard, "row", [(i, i ^ 1 << apart) for i in range(lax.axis_size("row"))])


def swap_cores(shard):
    return lax.ppermute(shard, "col", [(i, i ^ 1) for i in range(lax.axis_size("col"))])


def never(held, columns):
    row = held[:1, : min(columns, held.shape[1])]
    if columns > row.shape[1]:
        row = jnp.tile(row, (1, columns // row.shape[1]))
    return row != row


def after(value, held):
    if held is None:
        return value
    return jnp.where(never(held, value.shape[1]), -value, value)


class Broadcast:
    def __init__(self, reflectors, factors, owner, first_row, streams):
        size = lax.axis_size("col")
        self.me = lax.axis_index("col")
        self.first = self.me % 2 == 0
        self.owner = owner
        self.rows = reflectors.shape[0] - first_row
        self.width = factors.shape[0]
        part = (self.rows + self.width) // 2 // streams
        cut = [slice(k * part, (k + 1) * part) for k in range(streams)]

        def half(number):
            rows = lax.dynamic_slice_in_dim(
                reflectors, first_row + number * (self.rows // 2), self.rows // 2, 0
            )
            factor = lax.dynamic_slice_in_dim(factors, number * (self.width // 2), self.width // 2, 0)
            return jnp.concatenate([rows, factor], axis=0)

        mine = half(self.me % 2)
        other = half(1 - self.me % 2)
        self.mine, self.sent = [mine[c] for c in cut], [other[c] for c in cut]
        bits = [1 << k for k in range(1, size.bit_length() - 1)]
        turned = bits[len(bits) // 2 :] + bits[: len(bits) // 2]
        self.exchanges = [
            (
                [(i, i ^ (odd if i % 2 else even)) for i in range(size)],
                jnp.where(self.first, even, odd),
            )
            for even, odd in zip(bits, turned)
        ]
        self.bit = 1

    def begin(self, held=None):
        self.arrived = [swap_cores(after(s, held)) for s in self.sent]
        self.current = self.mine

    def select(self, held):
        keep = (self.me ^ self.owner) & self.bit == 0
        result = []
        for current, arrived in zip(self.current, self.arrived):
            if held is not None:
                keep = jnp.logical_or(keep, never(held, current.shape[1]))
            result.append(jnp.where(keep, current, arrived))
        self.current = result

    def exchange(self, number, held=None):
        self.select(held)
        pairs, self.bit = self.exchanges[number]
        self.arrived = [lax.ppermute(c, "col", pairs) for c in self.current]

    def end(self, held=None):
        self.select(held)
        other = [swap_cores(c) for c in self.current]
        self.arrived = other
        side_0 = jnp.concatenate([jnp.where(self.first, c, o) for c, o in zip(self.current, other)], axis=0)
        side_1 = jnp.concatenate([jnp.where(self.first, o, c) for c, o in zip(self.current, other)], axis=0)
        half = self.rows // 2
        block = jnp.concatenate([side_0[:half], side_1[:half]], axis=0)
        return block, jnp.concatenate([side_0[half:], side_1[half:]], axis=0)


def shards(slab, owner, leaf_reflectors, leaf_factors, tree_reflectors, tree_mixers):
    rows_dev, columns = slab.shape
    width = leaf_factors.shape[1]
    panels = owner.shape[0]
    levels = lax.axis_size("row").bit_length() - 1

    def bounds(panel_no):
        parts = CUTS[min(panel_no, len(CUTS) - 1)]
        edges = [0]
        for part in parts:
            edges.append(edges[-1] + columns * part // sum(parts))
        return list(zip(edges[:-1], edges[1:]))

    casts = [
        Broadcast(
            leaf_reflectors[p], leaf_factors[p], owner[p], p * width, 1 if p else STREAMS
        )
        for p in range(panels)
    ]
    blocks = [None] * panels
    tops = [None] * panels
    chunks = [{} for _ in range(panels)]
    edges = [bounds(p) for p in range(panels)]
    marks = {}
    lower = [slab]
    result = None

    def leaf(panel_no, held):
        block, factor = blocks[panel_no]
        if held is not None:
            block, _ = lax.optimization_barrier((block, held))
        matrix = lower[-1]
        scaled = dot_t(factor, dot_t(block, matrix))
        tops[panel_no] = matrix[:width] - dot(block[:width], scaled)
        lower.append(matrix[width:] - dot(block[width:], scaled))

    def head(panel_no, chunk):
        block, factor = blocks[panel_no]
        start, stop = edges[panel_no][chunk]
        part = lower[-1][:, start:stop]
        scaled = dot_t(factor, dot_t(block, part))
        return part[:width] - dot(block[:width], scaled)

    def send(panel_no, chunk, held):
        start, stop = edges[panel_no][chunk]
        piece = head(panel_no, chunk) if tops[panel_no] is None else tops[panel_no][:, start:stop]
        own = after(dot_t(tree_reflectors[panel_no, 0], piece), held)
        theirs = from_partner(own, 0)
        chunks[panel_no][chunk] = [piece, own, theirs, 0]
        marks[f"own{panel_no}.{chunk}"] = own
        marks[f"got{panel_no}.{chunk}"] = theirs

    def tree(panel_no, chunk, held):
        piece, own, theirs, level_no = chunks[panel_no][chunk]
        piece = piece - dot(tree_mixers[panel_no, level_no], after(own + theirs, held))
        own = dot_t(tree_reflectors[panel_no, level_no + 1], piece)
        theirs = from_partner(own, level_no + 1)
        chunks[panel_no][chunk] = [piece, own, theirs, level_no + 1]
        marks[f"up{panel_no}.{chunk}"] = own
        marks[f"gup{panel_no}.{chunk}"] = theirs

    def last(panel_no, chunk, held):
        nonlocal result
        if result is None:
            result = jnp.concatenate(tops + lower[-1:], axis=0)
        piece, own, theirs, level_no = chunks[panel_no][chunk]
        piece = piece - dot(tree_mixers[panel_no, level_no], after(own + theirs, held))
        marks[f"end{panel_no}.{chunk}"] = piece
        result = lax.dynamic_update_slice(result, piece, (panel_no * width, edges[panel_no][chunk][0]))

    for text, mark in PLAN:
        held = marks[mark] if mark else None
        name, numbers = text.rstrip("0123456789."), text[len(text.rstrip("0123456789.")) :].split(".")
        panel_no = int(numbers[0])
        if panel_no >= panels:
            continue
        if name == "begin":
            casts[panel_no].begin(held)
        elif name == "move":
            if int(numbers[1]) == 0:
                casts[panel_no].exchange(0, held)
                marks[f"arr{panel_no}.0"] = casts[panel_no].arrived[-1]
            else:
                for number in range(1, len(casts[panel_no].exchanges)):
                    casts[panel_no].exchange(number, held)
                marks[f"arr{panel_no}.1"] = casts[panel_no].arrived[-1]
        elif name == "end":
            blocks[panel_no] = casts[panel_no].end(held)
            marks[f"arr{panel_no}.2"] = casts[panel_no].arrived[-1]
        elif name == "leaf":
            leaf(panel_no, held)
        elif name == "send":
            send(panel_no, int(numbers[1]), held)
        elif name == "tree":
            for _ in range(levels - 1):
                tree(panel_no, int(numbers[1]), held)
        else:
            last(panel_no, int(numbers[1]), held)
    return result


def solution(mesh):
    return jax.shard_map(
        shards,
        mesh=mesh,
        in_specs=(
            P("row", "col"),
            P(),
            P(None, "row", "col"),
            P(None, "row", "col"),
            P(None, None, "row", None),
            P(None, None, "row", None),
        ),
        out_specs=P("row", "col"),
        check_vma=False,
    )
```

```python
import jax
import jax.numpy as jnp
from jax import lax
from jax.sharding import PartitionSpec as P

PRECISION = lax.Precision.HIGH
LEADING = (((0,), (0,)), ((), ()))
CUTS = ((1, 1, 1, 1), (1, 1))
STREAMS = 2
PLAN = (
    ("begin0", ""),
    ("move0.0", ""),
    ("move0.1", ""),
    ("end0", ""),
    ("send0.0", ""),
    ("leaf0", "own0.0"),
    ("send0.1", ""),
    ("send0.2", "got0.0"),
    ("send0.3", "got0.0"),
    ("begin1", ""),
    ("move1.0", "own0.0"),
    ("move1.1", ""),
    ("end1", ""),
    ("leaf1", ""),
    ("send1.0", ""),
    ("send1.1", "got1.0"),
    ("tree0.0", ""),
    ("tree0.1", "own0.3"),
    ("tree0.2", ""),
    ("tree0.3", "own1.0"),
    ("tree1.0", ""),
    ("tree1.1", ""),
    ("last0.0", ""),
    ("last0.1", ""),
    ("last0.2", ""),
    ("last0.3", ""),
    ("last1.0", ""),
    ("last1.1", ""),
)


def dot(a, b):
    return jnp.dot(a, b, precision=PRECISION, preferred_element_type=jnp.float32)


def dot_t(a, b):
    return lax.dot_general(a, b, LEADING, precision=PRECISION, preferred_element_type=jnp.float32)


def from_partner(shard, apart):
    return lax.ppermute(shard, "row", [(i, i ^ 1 << apart) for i in range(lax.axis_size("row"))])


def swap_cores(shard):
    return lax.ppermute(shard, "col", [(i, i ^ 1) for i in range(lax.axis_size("col"))])


def never(held, columns):
    row = held[:1, : min(columns, held.shape[1])]
    if columns > row.shape[1]:
        row = jnp.tile(row, (1, columns // row.shape[1]))
    return row != row


def after(value, held):
    if held is None:
        return value
    return jnp.where(never(held, value.shape[1]), -value, value)


class Broadcast:
    def __init__(self, reflectors, factors, owner, first_row, streams):
        size = lax.axis_size("col")
        self.me = lax.axis_index("col")
        self.first = self.me % 2 == 0
        self.owner = owner
        self.rows = reflectors.shape[0] - first_row
        self.width = factors.shape[0]
        part = (self.rows + self.width) // 2 // streams
        cut = [slice(k * part, (k + 1) * part) for k in range(streams)]

        def half(number):
            rows = lax.dynamic_slice_in_dim(
                reflectors, first_row + number * (self.rows // 2), self.rows // 2, 0
            )
            factor = lax.dynamic_slice_in_dim(factors, number * (self.width // 2), self.width // 2, 0)
            return jnp.concatenate([rows, factor], axis=0)

        mine = half(self.me % 2)
        other = half(1 - self.me % 2)
        self.mine, self.sent = [mine[c] for c in cut], [other[c] for c in cut]
        bits = [1 << k for k in range(1, size.bit_length() - 1)]
        turned = bits[len(bits) // 2 :] + bits[: len(bits) // 2]
        self.exchanges = [
            (
                [(i, i ^ (odd if i % 2 else even)) for i in range(size)],
                jnp.where(self.first, even, odd),
            )
            for even, odd in zip(bits, turned)
        ]
        self.bit = 1

    def begin(self, held=None):
        self.arrived = [swap_cores(after(s, held)) for s in self.sent]
        self.current = self.mine

    def select(self, held):
        keep = (self.me ^ self.owner) & self.bit == 0
        result = []
        for current, arrived in zip(self.current, self.arrived):
            if held is not None:
                keep = jnp.logical_or(keep, never(held, current.shape[1]))
            result.append(jnp.where(keep, current, arrived))
        self.current = result

    def exchange(self, number, held=None):
        self.select(held)
        pairs, self.bit = self.exchanges[number]
        self.arrived = [lax.ppermute(c, "col", pairs) for c in self.current]

    def end(self, held=None):
        self.select(held)
        other = [swap_cores(c) for c in self.current]
        self.arrived = other
        side_0 = jnp.concatenate([jnp.where(self.first, c, o) for c, o in zip(self.current, other)], axis=0)
        side_1 = jnp.concatenate([jnp.where(self.first, o, c) for c, o in zip(self.current, other)], axis=0)
        half = self.rows // 2
        block = jnp.concatenate([side_0[:half], side_1[:half]], axis=0)
        return block, jnp.concatenate([side_0[half:], side_1[half:]], axis=0)


def shards(slab, owner, leaf_reflectors, leaf_factors, tree_reflectors, tree_mixers):
    rows_dev, columns = slab.shape
    width = leaf_factors.shape[1]
    panels = owner.shape[0]
    levels = lax.axis_size("row").bit_length() - 1

    def bounds(panel_no):
        parts = CUTS[min(panel_no, len(CUTS) - 1)]
        edges = [0]
        for part in parts:
            edges.append(edges[-1] + columns * part // sum(parts))
        return list(zip(edges[:-1], edges[1:]))

    casts = [
        Broadcast(
            leaf_reflectors[p], leaf_factors[p], owner[p], p * width, 1 if p else STREAMS
        )
        for p in range(panels)
    ]
    blocks = [None] * panels
    tops = [None] * panels
    chunks = [{} for _ in range(panels)]
    edges = [bounds(p) for p in range(panels)]
    marks = {}
    lower = [slab]
    result = None

    def leaf(panel_no, held):
        block, factor = blocks[panel_no]
        if held is not None:
            block, _ = lax.optimization_barrier((block, held))
        matrix = lower[-1]
        scaled = dot_t(factor, dot_t(block, matrix))
        tops[panel_no] = matrix[:width] - dot(block[:width], scaled)
        lower.append(matrix[width:] - dot(block[width:], scaled))

    def head(panel_no, chunk):
        block, factor = blocks[panel_no]
        start, stop = edges[panel_no][chunk]
        part = after(lower[-1][:, start:stop], marks["arr0.0"])
        scaled = dot_t(factor, dot_t(block, part))
        return part[:width] - dot(block[:width], scaled)

    def send(panel_no, chunk, held):
        start, stop = edges[panel_no][chunk]
        piece = head(panel_no, chunk) if tops[panel_no] is None else tops[panel_no][:, start:stop]
        own = after(dot_t(tree_reflectors[panel_no, 0], piece), held)
        theirs = from_partner(own, 0)
        chunks[panel_no][chunk] = [piece, own, theirs, 0]
        marks[f"own{panel_no}.{chunk}"] = own
        marks[f"got{panel_no}.{chunk}"] = theirs

    def tree(panel_no, chunk, held):
        piece, own, theirs, level_no = chunks[panel_no][chunk]
        piece = piece - dot(tree_mixers[panel_no, level_no], after(own + theirs, held))
        own = dot_t(tree_reflectors[panel_no, level_no + 1], piece)
        theirs = from_partner(own, level_no + 1)
        chunks[panel_no][chunk] = [piece, own, theirs, level_no + 1]
        marks[f"up{panel_no}.{chunk}"] = own
        marks[f"gup{panel_no}.{chunk}"] = theirs

    def last(panel_no, chunk, held):
        nonlocal result
        if result is None:
            result = jnp.concatenate(tops + lower[-1:], axis=0)
        piece, own, theirs, level_no = chunks[panel_no][chunk]
        piece = piece - dot(tree_mixers[panel_no, level_no], after(own + theirs, held))
        marks[f"end{panel_no}.{chunk}"] = piece
        result = lax.dynamic_update_slice(result, piece, (panel_no * width, edges[panel_no][chunk][0]))

    for text, mark in PLAN:
        held = marks[mark] if mark else None
        name, numbers = text.rstrip("0123456789."), text[len(text.rstrip("0123456789.")) :].split(".")
        panel_no = int(numbers[0])
        if panel_no >= panels:
            continue
        if name == "begin":
            casts[panel_no].begin(held)
        elif name == "move":
            if int(numbers[1]) == 0:
                casts[panel_no].exchange(0, held)
                marks[f"arr{panel_no}.0"] = casts[panel_no].arrived[-1]
            else:
                for number in range(1, len(casts[panel_no].exchanges)):
                    casts[panel_no].exchange(number, held)
                marks[f"arr{panel_no}.1"] = casts[panel_no].arrived[-1]
        elif name == "end":
            blocks[panel_no] = casts[panel_no].end(held)
            marks[f"arr{panel_no}.2"] = casts[panel_no].arrived[-1]
        elif name == "leaf":
            leaf(panel_no, held)
        elif name == "send":
            send(panel_no, int(numbers[1]), held)
        elif name == "tree":
            for _ in range(levels - 1):
                tree(panel_no, int(numbers[1]), held)
        else:
            last(panel_no, int(numbers[1]), held)
    return result


def solution(mesh):
    return jax.shard_map(
        shards,
        mesh=mesh,
        in_specs=(
            P("row", "col"),
            P(),
            P(None, "row", "col"),
            P(None, "row", "col"),
            P(None, None, "row", None),
            P(None, None, "row", None),
        ),
        out_specs=P("row", "col"),
        check_vma=False,
    )
```

```python
import jax
import jax.numpy as jnp
from jax import lax
from jax.sharding import PartitionSpec as P

PRECISION = lax.Precision.HIGH
LEADING = (((0,), (0,)), ((), ()))
CUTS = ((1, 1, 1, 1), (1, 1))
STREAMS = 2
PLAN = (
    ("begin0", ""),
    ("move0.0", ""),
    ("move0.1", ""),
    ("end0", ""),
    ("send0.0", ""),
    ("leaf0", "own0.0"),
    ("send0.1", ""),
    ("send0.2", "got0.0"),
    ("send0.3", "got0.0"),
    ("begin1", "arr0.0"),
    ("move1.0", "own0.0"),
    ("move1.1", ""),
    ("end1", ""),
    ("leaf1", ""),
    ("send1.0", ""),
    ("send1.1", "got1.0"),
    ("tree0.0", ""),
    ("tree0.1", "own0.3"),
    ("tree0.2", ""),
    ("tree0.3", "own1.0"),
    ("tree1.0", ""),
    ("tree1.1", ""),
    ("last0.0", ""),
    ("last0.1", ""),
    ("last0.2", ""),
    ("last0.3", ""),
    ("last1.0", ""),
    ("last1.1", ""),
)


def dot(a, b):
    return jnp.dot(a, b, precision=PRECISION, preferred_element_type=jnp.float32)


def dot_t(a, b):
    return lax.dot_general(a, b, LEADING, precision=PRECISION, preferred_element_type=jnp.float32)


def from_partner(shard, apart):
    return lax.ppermute(shard, "row", [(i, i ^ 1 << apart) for i in range(lax.axis_size("row"))])


def swap_cores(shard):
    return lax.ppermute(shard, "col", [(i, i ^ 1) for i in range(lax.axis_size("col"))])


def never(held, columns):
    row = held[:1, : min(columns, held.shape[1])]
    if columns > row.shape[1]:
        row = jnp.tile(row, (1, columns // row.shape[1]))
    return row != row


def after(value, held):
    if held is None:
        return value
    return jnp.where(never(held, value.shape[1]), -value, value)


class Broadcast:
    def __init__(self, reflectors, factors, owner, first_row, streams):
        size = lax.axis_size("col")
        self.me = lax.axis_index("col")
        self.first = self.me % 2 == 0
        self.owner = owner
        self.rows = reflectors.shape[0] - first_row
        self.width = factors.shape[0]
        part = (self.rows + self.width) // 2 // streams
        cut = [slice(k * part, (k + 1) * part) for k in range(streams)]
        middle = first_row + self.rows // 2
        block_0 = jnp.concatenate([reflectors[first_row:middle], factors[: self.width // 2]], axis=0)
        block_1 = jnp.concatenate([reflectors[middle:], factors[self.width // 2 :]], axis=0)
        mine = jnp.where(self.first, block_0, block_1)
        other = jnp.where(self.first, block_1, block_0)
        self.mine, self.sent = [mine[c] for c in cut], [other[c] for c in cut]
        bits = [1 << k for k in range(1, size.bit_length() - 1)]
        turned = bits[len(bits) // 2 :] + bits[: len(bits) // 2]
        self.exchanges = [
            (
                [(i, i ^ (odd if i % 2 else even)) for i in range(size)],
                jnp.where(self.first, even, odd),
            )
            for even, odd in zip(bits, turned)
        ]
        self.bit = 1

    def begin(self, held=None):
        self.arrived = [swap_cores(after(s, held)) for s in self.sent]
        self.current = self.mine

    def select(self, held):
        keep = (self.me ^ self.owner) & self.bit == 0
        result = []
        for current, arrived in zip(self.current, self.arrived):
            if held is not None:
                keep = jnp.logical_or(keep, never(held, current.shape[1]))
            result.append(jnp.where(keep, current, arrived))
        self.current = result

    def exchange(self, number, held=None):
        self.select(held)
        pairs, self.bit = self.exchanges[number]
        self.arrived = [lax.ppermute(c, "col", pairs) for c in self.current]

    def end(self, held=None):
        self.select(held)
        other = [swap_cores(c) for c in self.current]
        self.arrived = other
        side_0 = jnp.concatenate([jnp.where(self.first, c, o) for c, o in zip(self.current, other)], axis=0)
        side_1 = jnp.concatenate([jnp.where(self.first, o, c) for c, o in zip(self.current, other)], axis=0)
        half = self.rows // 2
        block = jnp.concatenate([side_0[:half], side_1[:half]], axis=0)
        return block, jnp.concatenate([side_0[half:], side_1[half:]], axis=0)


def shards(slab, owner, leaf_reflectors, leaf_factors, tree_reflectors, tree_mixers):
    rows_dev, columns = slab.shape
    width = leaf_factors.shape[1]
    panels = owner.shape[0]
    levels = lax.axis_size("row").bit_length() - 1

    def bounds(panel_no):
        parts = CUTS[min(panel_no, len(CUTS) - 1)]
        edges = [0]
        for part in parts:
            edges.append(edges[-1] + columns * part // sum(parts))
        return list(zip(edges[:-1], edges[1:]))

    casts = [
        Broadcast(
            leaf_reflectors[p], leaf_factors[p], owner[p], p * width, 1 if p else STREAMS
        )
        for p in range(panels)
    ]
    blocks = [None] * panels
    tops = [None] * panels
    chunks = [{} for _ in range(panels)]
    edges = [bounds(p) for p in range(panels)]
    marks = {}
    lower = [slab]
    result = None

    def leaf(panel_no, held):
        block, factor = blocks[panel_no]
        if held is not None:
            block, _ = lax.optimization_barrier((block, held))
        matrix = lower[-1]
        scaled = dot_t(factor, dot_t(block, matrix))
        tops[panel_no] = matrix[:width] - dot(block[:width], scaled)
        lower.append(matrix[width:] - dot(block[width:], scaled))

    def head(panel_no, chunk):
        block, factor = blocks[panel_no]
        start, stop = edges[panel_no][chunk]
        part = after(lower[-1][:, start:stop], marks["arr0.0"])
        scaled = dot_t(factor, dot_t(block, part))
        return part[:width] - dot(block[:width], scaled)

    def send(panel_no, chunk, held):
        start, stop = edges[panel_no][chunk]
        piece = head(panel_no, chunk) if tops[panel_no] is None else tops[panel_no][:, start:stop]
        own = after(dot_t(tree_reflectors[panel_no, 0], piece), held)
        theirs = from_partner(own, 0)
        chunks[panel_no][chunk] = [piece, own, theirs, 0]
        marks[f"own{panel_no}.{chunk}"] = own
        marks[f"got{panel_no}.{chunk}"] = theirs

    def tree(panel_no, chunk, held):
        piece, own, theirs, level_no = chunks[panel_no][chunk]
        piece = piece - dot(tree_mixers[panel_no, level_no], after(own + theirs, held))
        own = dot_t(tree_reflectors[panel_no, level_no + 1], piece)
        theirs = from_partner(own, level_no + 1)
        chunks[panel_no][chunk] = [piece, own, theirs, level_no + 1]
        marks[f"up{panel_no}.{chunk}"] = own
        marks[f"gup{panel_no}.{chunk}"] = theirs

    def last(panel_no, chunk, held):
        nonlocal result
        if result is None:
            result = jnp.concatenate(tops + lower[-1:], axis=0)
        piece, own, theirs, level_no = chunks[panel_no][chunk]
        piece = piece - dot(tree_mixers[panel_no, level_no], after(own + theirs, held))
        marks[f"end{panel_no}.{chunk}"] = piece
        result = lax.dynamic_update_slice(result, piece, (panel_no * width, edges[panel_no][chunk][0]))

    for text, mark in PLAN:
        held = marks[mark] if mark else None
        name, numbers = text.rstrip("0123456789."), text[len(text.rstrip("0123456789.")) :].split(".")
        panel_no = int(numbers[0])
        if panel_no >= panels:
            continue
        if name == "begin":
            casts[panel_no].begin(held)
        elif name == "move":
            if int(numbers[1]) == 0:
                casts[panel_no].exchange(0, held)
                marks[f"arr{panel_no}.0"] = casts[panel_no].arrived[-1]
            else:
                for number in range(1, len(casts[panel_no].exchanges)):
                    casts[panel_no].exchange(number, held)
                marks[f"arr{panel_no}.1"] = casts[panel_no].arrived[-1]
        elif name == "end":
            blocks[panel_no] = casts[panel_no].end(held)
            marks[f"arr{panel_no}.2"] = casts[panel_no].arrived[-1]
        elif name == "leaf":
            leaf(panel_no, held)
        elif name == "send":
            send(panel_no, int(numbers[1]), held)
        elif name == "tree":
            for _ in range(levels - 1):
                tree(panel_no, int(numbers[1]), held)
        else:
            last(panel_no, int(numbers[1]), held)
    return result


def solution(mesh):
    return jax.shard_map(
        shards,
        mesh=mesh,
        in_specs=(
            P("row", "col"),
            P(),
            P(None, "row", "col"),
            P(None, "row", "col"),
            P(None, None, "row", None),
            P(None, None, "row", None),
        ),
        out_specs=P("row", "col"),
        check_vma=False,
    )
```

```python
import jax
import jax.numpy as jnp
from jax import lax
from jax.sharding import PartitionSpec as P

PRECISION = lax.Precision.HIGH
LEADING = (((0,), (0,)), ((), ()))
CUTS = ((1, 1, 1, 1), (1, 1))
STREAMS = 2
PLAN = (
    ("begin0", ""),
    ("move0.0", ""),
    ("move0.1", ""),
    ("end0", ""),
    ("send0.0", ""),
    ("leaf0", "own0.0"),
    ("send0.1", ""),
    ("send0.2", "got0.0"),
    ("send0.3", "got0.0"),
    ("begin1", "arr0.0"),
    ("move1.0", "own0.0"),
    ("tree0.0", ""),
    ("move1.1", "up0.0"),
    ("end1", ""),
    ("leaf1", ""),
    ("send1.0", ""),
    ("send1.1", "got1.0"),
    ("tree0.1", "own0.3"),
    ("tree0.2", ""),
    ("tree0.3", "own1.0"),
    ("tree1.0", ""),
    ("tree1.1", ""),
    ("last0.0", ""),
    ("last0.1", ""),
    ("last0.2", ""),
    ("last0.3", ""),
    ("last1.0", ""),
    ("last1.1", ""),
)


def dot(a, b):
    return jnp.dot(a, b, precision=PRECISION, preferred_element_type=jnp.float32)


def dot_t(a, b):
    return lax.dot_general(a, b, LEADING, precision=PRECISION, preferred_element_type=jnp.float32)


def from_partner(shard, apart):
    return lax.ppermute(shard, "row", [(i, i ^ 1 << apart) for i in range(lax.axis_size("row"))])


def swap_cores(shard):
    return lax.ppermute(shard, "col", [(i, i ^ 1) for i in range(lax.axis_size("col"))])


def never(held, columns):
    row = held[:1, : min(columns, held.shape[1])]
    if columns > row.shape[1]:
        row = jnp.tile(row, (1, columns // row.shape[1]))
    return row != row


def after(value, held):
    if held is None:
        return value
    return jnp.where(never(held, value.shape[1]), -value, value)


class Broadcast:
    def __init__(self, reflectors, factors, owner, first_row, streams):
        size = lax.axis_size("col")
        self.me = lax.axis_index("col")
        self.first = self.me % 2 == 0
        self.owner = owner
        self.rows = reflectors.shape[0] - first_row
        self.width = factors.shape[0]
        part = (self.rows + self.width) // 2 // streams
        cut = [slice(k * part, (k + 1) * part) for k in range(streams)]
        middle = first_row + self.rows // 2
        block_0 = jnp.concatenate([reflectors[first_row:middle], factors[: self.width // 2]], axis=0)
        block_1 = jnp.concatenate([reflectors[middle:], factors[self.width // 2 :]], axis=0)
        mine = jnp.where(self.first, block_0, block_1)
        other = jnp.where(self.first, block_1, block_0)
        self.mine, self.sent = [mine[c] for c in cut], [other[c] for c in cut]
        bits = [1 << k for k in range(1, size.bit_length() - 1)]
        turned = bits[len(bits) // 2 :] + bits[: len(bits) // 2]
        self.exchanges = [
            (
                [(i, i ^ (odd if i % 2 else even)) for i in range(size)],
                jnp.where(self.first, even, odd),
            )
            for even, odd in zip(bits, turned)
        ]
        self.bit = 1

    def begin(self, held=None):
        self.arrived = [swap_cores(after(s, held)) for s in self.sent]
        self.current = self.mine

    def select(self, held):
        keep = (self.me ^ self.owner) & self.bit == 0
        result = []
        for current, arrived in zip(self.current, self.arrived):
            if held is not None:
                keep = jnp.logical_or(keep, never(held, current.shape[1]))
            result.append(jnp.where(keep, current, arrived))
        self.current = result

    def exchange(self, number, held=None):
        self.select(held)
        pairs, self.bit = self.exchanges[number]
        self.arrived = [lax.ppermute(c, "col", pairs) for c in self.current]

    def end(self, held=None):
        self.select(held)
        other = [swap_cores(c) for c in self.current]
        self.arrived = other
        side_0 = jnp.concatenate([jnp.where(self.first, c, o) for c, o in zip(self.current, other)], axis=0)
        side_1 = jnp.concatenate([jnp.where(self.first, o, c) for c, o in zip(self.current, other)], axis=0)
        half = self.rows // 2
        block = jnp.concatenate([side_0[:half], side_1[:half]], axis=0)
        return block, jnp.concatenate([side_0[half:], side_1[half:]], axis=0)


def shards(slab, owner, leaf_reflectors, leaf_factors, tree_reflectors, tree_mixers):
    rows_dev, columns = slab.shape
    width = leaf_factors.shape[1]
    panels = owner.shape[0]
    levels = lax.axis_size("row").bit_length() - 1

    def bounds(panel_no):
        parts = CUTS[min(panel_no, len(CUTS) - 1)]
        edges = [0]
        for part in parts:
            edges.append(edges[-1] + columns * part // sum(parts))
        return list(zip(edges[:-1], edges[1:]))

    casts = [
        Broadcast(
            leaf_reflectors[p], leaf_factors[p], owner[p], p * width, 1 if p else STREAMS
        )
        for p in range(panels)
    ]
    blocks = [None] * panels
    tops = [None] * panels
    chunks = [{} for _ in range(panels)]
    edges = [bounds(p) for p in range(panels)]
    marks = {}
    lower = [slab]
    result = None

    def leaf(panel_no, held):
        block, factor = blocks[panel_no]
        if held is not None:
            block, _ = lax.optimization_barrier((block, held))
        matrix = lower[-1]
        scaled = dot_t(factor, dot_t(block, matrix))
        tops[panel_no] = matrix[:width] - dot(block[:width], scaled)
        lower.append(matrix[width:] - dot(block[width:], scaled))

    def head(panel_no, chunk):
        block, factor = blocks[panel_no]
        start, stop = edges[panel_no][chunk]
        part = after(lower[-1][:, start:stop], marks["arr0.0"])
        scaled = dot_t(factor, dot_t(block, part))
        return part[:width] - dot(block[:width], scaled)

    def send(panel_no, chunk, held):
        start, stop = edges[panel_no][chunk]
        piece = head(panel_no, chunk) if tops[panel_no] is None else tops[panel_no][:, start:stop]
        own = after(dot_t(tree_reflectors[panel_no, 0], piece), held)
        theirs = from_partner(own, 0)
        chunks[panel_no][chunk] = [piece, own, theirs, 0]
        marks[f"own{panel_no}.{chunk}"] = own
        marks[f"got{panel_no}.{chunk}"] = theirs

    def tree(panel_no, chunk, held):
        piece, own, theirs, level_no = chunks[panel_no][chunk]
        piece = piece - dot(tree_mixers[panel_no, level_no], after(own + theirs, held))
        own = dot_t(tree_reflectors[panel_no, level_no + 1], piece)
        theirs = from_partner(own, level_no + 1)
        chunks[panel_no][chunk] = [piece, own, theirs, level_no + 1]
        marks[f"up{panel_no}.{chunk}"] = own
        marks[f"gup{panel_no}.{chunk}"] = theirs

    def last(panel_no, chunk, held):
        nonlocal result
        if result is None:
            result = jnp.concatenate(tops + lower[-1:], axis=0)
        piece, own, theirs, level_no = chunks[panel_no][chunk]
        piece = piece - dot(tree_mixers[panel_no, level_no], after(own + theirs, held))
        marks[f"end{panel_no}.{chunk}"] = piece
        result = lax.dynamic_update_slice(result, piece, (panel_no * width, edges[panel_no][chunk][0]))

    for text, mark in PLAN:
        held = marks[mark] if mark else None
        name, numbers = text.rstrip("0123456789."), text[len(text.rstrip("0123456789.")) :].split(".")
        panel_no = int(numbers[0])
        if panel_no >= panels:
            continue
        if name == "begin":
            casts[panel_no].begin(held)
        elif name == "move":
            if int(numbers[1]) == 0:
                casts[panel_no].exchange(0, held)
                marks[f"arr{panel_no}.0"] = casts[panel_no].arrived[-1]
            else:
                for number in range(1, len(casts[panel_no].exchanges)):
                    casts[panel_no].exchange(number, held)
                marks[f"arr{panel_no}.1"] = casts[panel_no].arrived[-1]
        elif name == "end":
            blocks[panel_no] = casts[panel_no].end(held)
            marks[f"arr{panel_no}.2"] = casts[panel_no].arrived[-1]
        elif name == "leaf":
            leaf(panel_no, held)
        elif name == "send":
            send(panel_no, int(numbers[1]), held)
        elif name == "tree":
            for _ in range(levels - 1):
                tree(panel_no, int(numbers[1]), held)
        else:
            last(panel_no, int(numbers[1]), held)
    return result


def solution(mesh):
    return jax.shard_map(
        shards,
        mesh=mesh,
        in_specs=(
            P("row", "col"),
            P(),
            P(None, "row", "col"),
            P(None, "row", "col"),
            P(None, None, "row", None),
            P(None, None, "row", None),
        ),
        out_specs=P("row", "col"),
        check_vma=False,
    )
```

```python
import jax
import jax.numpy as jnp
from jax import lax
from jax.sharding import PartitionSpec as P

PRECISION = lax.Precision.HIGH
LEADING = (((0,), (0,)), ((), ()))
CUTS = ((1, 1, 1, 1), (1, 1))
STREAMS = 2
PLAN = (
    ("begin0", ""),
    ("move0.0", ""),
    ("move0.1", ""),
    ("end0", ""),
    ("send0.0", ""),
    ("leaf0", "own0.0"),
    ("send0.1", ""),
    ("send0.2", "got0.0"),
    ("send0.3", "got0.1"),
    ("begin1", "arr0.0"),
    ("move1.0", "own0.0"),
    ("move1.1", ""),
    ("end1", ""),
    ("leaf1", ""),
    ("send1.0", ""),
    ("send1.1", "got1.0"),
    ("tree0.0", ""),
    ("tree0.1", "own0.2"),
    ("tree0.2", ""),
    ("tree0.3", "own1.0"),
    ("tree1.0", ""),
    ("tree1.1", ""),
    ("last0.0", ""),
    ("last0.1", ""),
    ("last0.2", ""),
    ("last0.3", ""),
    ("last1.0", ""),
    ("last1.1", ""),
)


def dot(a, b):
    return jnp.dot(a, b, precision=PRECISION, preferred_element_type=jnp.float32)


def dot_t(a, b):
    return lax.dot_general(a, b, LEADING, precision=PRECISION, preferred_element_type=jnp.float32)


def from_partner(shard, apart):
    return lax.ppermute(shard, "row", [(i, i ^ 1 << apart) for i in range(lax.axis_size("row"))])


def swap_cores(shard):
    return lax.ppermute(shard, "col", [(i, i ^ 1) for i in range(lax.axis_size("col"))])


def never(held, columns):
    row = held[:1, : min(columns, held.shape[1])]
    if columns > row.shape[1]:
        row = jnp.tile(row, (1, columns // row.shape[1]))
    return row != row


def after(value, held):
    if held is None:
        return value
    return jnp.where(never(held, value.shape[1]), -value, value)


class Broadcast:
    def __init__(self, reflectors, factors, owner, first_row, streams):
        size = lax.axis_size("col")
        self.me = lax.axis_index("col")
        self.first = self.me % 2 == 0
        self.owner = owner
        self.rows = reflectors.shape[0] - first_row
        self.width = factors.shape[0]
        part = (self.rows + self.width) // 2 // streams
        cut = [slice(k * part, (k + 1) * part) for k in range(streams)]
        middle = first_row + self.rows // 2
        block_0 = jnp.concatenate([reflectors[first_row:middle], factors[: self.width // 2]], axis=0)
        block_1 = jnp.concatenate([reflectors[middle:], factors[self.width // 2 :]], axis=0)
        mine = jnp.where(self.first, block_0, block_1)
        other = jnp.where(self.first, block_1, block_0)
        self.mine, self.sent = [mine[c] for c in cut], [other[c] for c in cut]
        bits = [1 << k for k in range(1, size.bit_length() - 1)]
        turned = bits[len(bits) // 2 :] + bits[: len(bits) // 2]
        self.exchanges = [
            (
                [(i, i ^ (odd if i % 2 else even)) for i in range(size)],
                jnp.where(self.first, even, odd),
            )
            for even, odd in zip(bits, turned)
        ]
        self.bit = 1

    def begin(self, held=None):
        self.arrived = [swap_cores(after(s, held)) for s in self.sent]
        self.current = self.mine

    def select(self, held):
        keep = (self.me ^ self.owner) & self.bit == 0
        result = []
        for current, arrived in zip(self.current, self.arrived):
            if held is not None:
                keep = jnp.logical_or(keep, never(held, current.shape[1]))
            result.append(jnp.where(keep, current, arrived))
        self.current = result

    def exchange(self, number, held=None):
        self.select(held)
        pairs, self.bit = self.exchanges[number]
        self.arrived = [lax.ppermute(c, "col", pairs) for c in self.current]

    def end(self, held=None):
        self.select(held)
        other = [swap_cores(c) for c in self.current]
        self.arrived = other
        side_0 = jnp.concatenate([jnp.where(self.first, c, o) for c, o in zip(self.current, other)], axis=0)
        side_1 = jnp.concatenate([jnp.where(self.first, o, c) for c, o in zip(self.current, other)], axis=0)
        half = self.rows // 2
        block = jnp.concatenate([side_0[:half], side_1[:half]], axis=0)
        return block, jnp.concatenate([side_0[half:], side_1[half:]], axis=0)


def shards(slab, owner, leaf_reflectors, leaf_factors, tree_reflectors, tree_mixers):
    rows_dev, columns = slab.shape
    width = leaf_factors.shape[1]
    panels = owner.shape[0]
    levels = lax.axis_size("row").bit_length() - 1

    def bounds(panel_no):
        parts = CUTS[min(panel_no, len(CUTS) - 1)]
        edges = [0]
        for part in parts:
            edges.append(edges[-1] + columns * part // sum(parts))
        return list(zip(edges[:-1], edges[1:]))

    casts = [
        Broadcast(
            leaf_reflectors[p], leaf_factors[p], owner[p], p * width, 1 if p else STREAMS
        )
        for p in range(panels)
    ]
    blocks = [None] * panels
    tops = [None] * panels
    chunks = [{} for _ in range(panels)]
    edges = [bounds(p) for p in range(panels)]
    marks = {}
    lower = [slab]
    result = None

    def leaf(panel_no, held):
        block, factor = blocks[panel_no]
        if held is not None:
            block, _ = lax.optimization_barrier((block, held))
        matrix = lower[-1]
        scaled = dot_t(factor, dot_t(block, matrix))
        tops[panel_no] = matrix[:width] - dot(block[:width], scaled)
        lower.append(matrix[width:] - dot(block[width:], scaled))

    def head(panel_no, chunk):
        block, factor = blocks[panel_no]
        start, stop = edges[panel_no][chunk]
        part = after(lower[-1][:, start:stop], marks["arr0.0"])
        scaled = dot_t(factor, dot_t(block, part))
        return part[:width] - dot(block[:width], scaled)

    def send(panel_no, chunk, held):
        start, stop = edges[panel_no][chunk]
        piece = head(panel_no, chunk) if tops[panel_no] is None else tops[panel_no][:, start:stop]
        own = after(dot_t(tree_reflectors[panel_no, 0], piece), held)
        theirs = from_partner(own, 0)
        chunks[panel_no][chunk] = [piece, own, theirs, 0]
        marks[f"own{panel_no}.{chunk}"] = own
        marks[f"got{panel_no}.{chunk}"] = theirs

    def tree(panel_no, chunk, held):
        piece, own, theirs, level_no = chunks[panel_no][chunk]
        piece = piece - dot(tree_mixers[panel_no, level_no], after(own + theirs, held))
        own = dot_t(tree_reflectors[panel_no, level_no + 1], piece)
        theirs = from_partner(own, level_no + 1)
        chunks[panel_no][chunk] = [piece, own, theirs, level_no + 1]
        marks[f"up{panel_no}.{chunk}"] = own
        marks[f"gup{panel_no}.{chunk}"] = theirs

    def last(panel_no, chunk, held):
        nonlocal result
        if result is None:
            result = jnp.concatenate(tops + lower[-1:], axis=0)
        piece, own, theirs, level_no = chunks[panel_no][chunk]
        piece = piece - dot(tree_mixers[panel_no, level_no], after(own + theirs, held))
        marks[f"end{panel_no}.{chunk}"] = piece
        result = lax.dynamic_update_slice(result, piece, (panel_no * width, edges[panel_no][chunk][0]))

    for text, mark in PLAN:
        held = marks[mark] if mark else None
        name, numbers = text.rstrip("0123456789."), text[len(text.rstrip("0123456789.")) :].split(".")
        panel_no = int(numbers[0])
        if panel_no >= panels:
            continue
        if name == "begin":
            casts[panel_no].begin(held)
        elif name == "move":
            if int(numbers[1]) == 0:
                casts[panel_no].exchange(0, held)
                marks[f"arr{panel_no}.0"] = casts[panel_no].arrived[-1]
            else:
                for number in range(1, len(casts[panel_no].exchanges)):
                    casts[panel_no].exchange(number, held)
                marks[f"arr{panel_no}.1"] = casts[panel_no].arrived[-1]
        elif name == "end":
            blocks[panel_no] = casts[panel_no].end(held)
            marks[f"arr{panel_no}.2"] = casts[panel_no].arrived[-1]
        elif name == "leaf":
            leaf(panel_no, held)
        elif name == "send":
            send(panel_no, int(numbers[1]), held)
        elif name == "tree":
            for _ in range(levels - 1):
                tree(panel_no, int(numbers[1]), held)
        else:
            last(panel_no, int(numbers[1]), held)
    return result


def solution(mesh):
    return jax.shard_map(
        shards,
        mesh=mesh,
        in_specs=(
            P("row", "col"),
            P(),
            P(None, "row", "col"),
            P(None, "row", "col"),
            P(None, None, "row", None),
            P(None, None, "row", None),
        ),
        out_specs=P("row", "col"),
        check_vma=False,
    )
```
